32 devices in a mesh: gx: 8 (over y, x, core), row: 4 (over z).
Axes of the slice: x: 2, y: 2, z: 4, core: 2. Of those that a mesh axis runs over, the one named last changes fastest.
Arguments:
- amplitudes: float32 [128, 4096], P('gx', 'row'), may hold values from -6 to 6
- integrals: float32 [4096, 16384], P('row', 'gx'), may hold values from -0.1875 to 0.1875
- cd_irrep: int32 [32], P('row'), may hold values from 0 to 7
- ab_irrep: int32 [128], P('gx'), may hold values from 0 to 7
- allowed: int32 [8, 8], replicated, may hold values 0 or 1
- pair_occ: int32 [128, 2], P(('gx', 'row')), may hold values from 0 to 99
- occ_energy: float32 [100], replicated, may hold values from -1 to -0.25
- ab_energy: float32 [16384], replicated, may hold values from 1 to 4
Outputs:
- residual: float32 [128, 16384], P(('gx', 'row'))
- update: float32 [128, 16384], P(('gx', 'row'))
The draws below stay inside these ranges and needn't reach their ends.
All inputs are finite; a program needn't handle non-finite values.
Results may differ from the reference program's by a relative error of at most 0.000071.
Values sent between devices are 32-bit elements; how exact they have to be, the bound alone decides.
A program may use at most 128 MiB of HBM per device.

```python
import jax
import jax.numpy as jnp
from jax import lax

C = 4096
BLK = 128
NIRR = 8
NOCC = 100
AB_DEV = 2048
P_SIZE = 128
A = 16384
NCB = 32
NAB = 128
N_GX = 8


def set_ends(entries, stream_key, least, high):
    longest = entries.shape.index(max(entries.shape))
    spots = []
    for shift in (0, 1):
        where = [jax.random.randint(jax.random.fold_in(stream_key, axis), (), 0, length) for axis, length in enumerate(entries.shape)]
        where[longest] = (where[longest] + shift) % entries.shape[longest]
        spots.append(tuple(where))
    return entries.at[spots[0]].set(least).at[spots[1]].set(high)


def block_levels(own_key, dims, shards, least, high):
    loudness = 1.0
    for axis_at, blocks in shards:
        draws = jax.random.uniform(jax.random.fold_in(jax.random.fold_in(own_key, 6), axis_at), (blocks,), jnp.float32, least / len(shards), high / len(shards))
        loudness = loudness * jnp.repeat(jnp.exp(draws), dims[axis_at] // blocks).reshape((-1,) + (1,) * (len(dims) - 1 - axis_at))
    return loudness


def centred(rng, dims, scale, limit, pieces=(), kind=jnp.bfloat16):
    entries = scale * jax.random.normal(rng, dims, jnp.float32)
    if pieces:
        entries = entries * block_levels(rng, dims, pieces, -0.22, 0.18)
    return jnp.clip(entries, -limit, limit).astype(kind)


def setup_inputs(seed: int = 0) -> dict:
    key_list = jax.random.split(jax.random.key(seed), 9)
    return {
        "amplitudes": centred(key_list[0], (P_SIZE, C), 1.0, 6.0, ((0, 8), (1, 4)), jnp.float32),
        "integrals": centred(key_list[1], (C, A), (C // 4) ** -0.5, 0.1875, ((0, 4), (1, 8)), jnp.float32),
        "cd_irrep": set_ends(jax.random.randint(key_list[2], (NCB,), 0, NIRR), jax.random.fold_in(key_list[2], 1), 0, NIRR - 1).astype(jnp.int32),
        "ab_irrep": set_ends(jax.random.randint(key_list[3], (NAB,), 0, NIRR), jax.random.fold_in(key_list[3], 1), 0, NIRR - 1).astype(jnp.int32),
        "allowed": set_ends((jax.random.randint(key_list[4], (NIRR, NIRR), 0, 4) < 1).astype(jnp.int32), jax.random.fold_in(key_list[4], 1), 0, 1),
        "pair_occ": set_ends(jax.random.randint(key_list[5], (P_SIZE, 2), 0, NOCC), jax.random.fold_in(key_list[5], 1), 0, NOCC - 1).astype(jnp.int32),
        "occ_energy": jnp.clip(jax.random.uniform(key_list[6], (NOCC,), jnp.float32, -1.0, -0.25), -1.0, -0.25),
        "ab_energy": jnp.clip(jax.random.uniform(key_list[7], (A,), jnp.float32, 1.0, 4.0), 1.0, 4.0),
    }


def reference(amplitudes, integrals, cd_irrep, ab_irrep, allowed, pair_occ, occ_energy, ab_energy):
    block_mask = allowed[cd_irrep[:, None], ab_irrep[None, :]].astype(jnp.float32)
    ab_blocks = AB_DEV // BLK

    def one_slab(index):
        columns = lax.dynamic_slice_in_dim(integrals, index * AB_DEV, AB_DEV, 1)
        mask_part = lax.dynamic_slice_in_dim(block_mask, index * ab_blocks, ab_blocks, 1)
        effective = (columns.reshape(NCB, BLK, ab_blocks, BLK) * mask_part[:, None, :, None]).reshape(C, AB_DEV)
        return jnp.dot(amplitudes, effective, precision=lax.Precision.HIGHEST, preferred_element_type=jnp.float32)

    slabs = lax.map(one_slab, jnp.arange(N_GX, dtype=jnp.int32))
    residual = slabs.transpose(1, 0, 2).reshape(P_SIZE, A)
    pair_energy = occ_energy[pair_occ[:, 0]] + occ_energy[pair_occ[:, 1]]
    update = residual / (ab_energy[None, :] - pair_energy[:, None])
    return residual, update
```

```python
import functools

import jax
import jax.numpy as jnp
from jax import lax
from jax.experimental import pallas as pl
from jax.experimental.pallas import tpu as pltpu
from jax.sharding import PartitionSpec as P

BLK = 128
MESH = pl.DeviceIdType.MESH
VMEM_BUDGET = 48 * 2**20


def plain_body(amplitudes, integrals, cd_irrep, ab_irrep, allowed, pair_occ, occ_energy, ab_energy):
    irrep_labels = jnp.arange(allowed.shape[0], dtype=jnp.int32)
    cd_onehot = (cd_irrep[:, None] == irrep_labels[None, :]).astype(jnp.float32)
    ab_onehot = (ab_irrep[:, None] == irrep_labels[None, :]).astype(jnp.float32)
    irrep_table = allowed.astype(jnp.float32)
    block_mask = jnp.dot(
        jnp.dot(cd_onehot, irrep_table, precision=lax.Precision.HIGHEST),
        ab_onehot.T,
        precision=lax.Precision.HIGHEST,
    )
    cd_rows, ab_cols = integrals.shape
    effective = (
        integrals.reshape(cd_rows // BLK, BLK, ab_cols // BLK, BLK) * block_mask[:, None, :, None]
    ).reshape(cd_rows, ab_cols)
    partial_value = jnp.dot(
        lax.all_gather(amplitudes, "gx", axis=0, tiled=True),
        effective,
        precision=lax.Precision.HIGHEST,
        preferred_element_type=jnp.float32,
    )
    arrived = lax.all_to_all(partial_value, "gx", split_axis=0, concat_axis=1, tiled=True)
    residual = lax.psum_scatter(arrived, "row", scatter_dimension=0, tiled=True)
    occ_labels = jnp.arange(occ_energy.shape[0], dtype=jnp.int32)
    pair_onehot = (pair_occ[:, :, None] == occ_labels[None, None, :]).astype(jnp.float32)
    pair_energy = jnp.sum(pair_onehot * occ_energy[None, None, :], axis=(1, 2))
    update = residual / (ab_energy[None, :] - pair_energy[:, None])
    return (residual, update)


def kernel(
    N, Z, T, W,
    amp, integ, cd, ab, allowed, pair_occ, occ, ab_energy,
    res_out, upd_out,
    raw, wh, wl, gathered, ordered, a2, own, arrive, fin, landed,
    isem, ag_send, ag_recv, relay_send, zsend, zrecv, xsend, xrecv,
):
    g = lax.axis_index("gx")
    z = lax.axis_index("row")
    rows, K = amp.shape
    PP = rows * N
    pk = rows // Z
    partner = g + 1 - 2 * lax.rem(g, 2)
    parity = lax.rem(g, 2)

    def load(t):
        cols = pl.ds(pl.multiple_of(t * W, W), W)
        return pltpu.make_async_copy(integ.at[:, cols], raw.at[t], isem.at[t])

    for t in range(T):
        load(t).start()

    barrier = pltpu.get_barrier_semaphore()
    for j in range(1, N):
        pl.semaphore_signal(barrier, inc=1, device_id={"gx": lax.rem(g + j, N)}, device_id_type=MESH)

    @pl.when(z > 0)
    def _():
        pl.semaphore_signal(barrier, inc=1, device_id={"row": z - 1}, device_id_type=MESH)

    @pl.when(z < Z - 1)
    def _():
        pl.semaphore_signal(barrier, inc=1, device_id={"row": z + 1}, device_id_type=MESH)

    nearby = jnp.where(z > 0, 1, 0) + jnp.where(z < Z - 1, 1, 0)
    pl.semaphore_wait(barrier, N - 1 + nearby)

    def send_own(peer):
        return pltpu.make_async_remote_copy(
            src_ref=amp, dst_ref=gathered.at[g], send_sem=ag_send.at[peer], recv_sem=ag_recv.at[g],
            device_id={"gx": peer}, device_id_type=MESH)

    def relay(s):
        return pltpu.make_async_remote_copy(
            src_ref=gathered.at[s], dst_ref=gathered.at[s], send_sem=relay_send.at[s], recv_sem=ag_recv.at[s],
            device_id={"gx": partner}, device_id_type=MESH)

    like = [lax.rem(g + 2 * j, N) for j in range(N // 2 - 1, 0, -1)]
    for peer in like:
        send_own(peer).start()
    send_own(partner).start()
    gathered[g] = amp[...]

    KB = K // BLK
    WB = W // BLK

    def split(t, carry):
        load(t).wait()
        for b in range(KB):
            for j in range(WB):
                m = allowed[cd[b], ab[t * WB + j]].astype(jnp.float32)
                x = raw[t, b * BLK:(b + 1) * BLK, j * BLK:(j + 1) * BLK] * m
                hi = x.astype(jnp.bfloat16)
                wh[t, b * BLK:(b + 1) * BLK, j * BLK:(j + 1) * BLK] = hi
                wl[t, b * BLK:(b + 1) * BLK, j * BLK:(j + 1) * BLK] = (x - hi.astype(jnp.float32)).astype(jnp.bfloat16)
        return carry

    lax.fori_loop(0, T, split, 0)

    for s in like[::-1]:
        relay(s).wait_recv()
        relay(s).start()
    relay(partner).wait_recv()
    for j in range(1, N // 2):
        relay(lax.rem(partner + 2 * j, N)).wait_recv()

    for r in range(Z):
        for s in range(N):
            at = r * N * pk + s * pk
            ordered[at:at + pk, :] = gathered[s, r * pk:(r + 1) * pk, :]
    x = ordered[...]
    hi = x.astype(jnp.bfloat16)
    a2[0:PP, :] = hi
    a2[PP:2 * PP, :] = (x - hi.astype(jnp.float32)).astype(jnp.bfloat16)

    RP = N * pk

    def send_z(d, t, up):
        to = z + 1 if up else z - 1
        side = 0 if up else 1
        return pltpu.make_async_remote_copy(
            src_ref=own.at[d, t], dst_ref=arrive.at[side, d, t], send_sem=zsend.at[d, t],
            recv_sem=zrecv.at[side, d, t], device_id={"row": to}, device_id_type=MESH)

    def compute(t, carry):
        both = jnp.dot(a2[...], wh[t], preferred_element_type=jnp.float32)
        tail = jnp.dot(a2[0:PP, :], wl[t], preferred_element_type=jnp.float32)
        total = both[0:PP] + both[PP:2 * PP] + tail
        for d in range(Z):
            own[d, t] = total[d * RP:(d + 1) * RP, :]

        @pl.when(z == 0)
        def _():
            send_z(Z - 1, t, True).start()

        @pl.when(z == Z - 1)
        def _():
            send_z(0, t, False).start()
        return carry

    lax.fori_loop(0, T, compute, 0)

    def pass_on(d, t, up):
        side = 0 if up else 1
        send_z(d, t, up).wait_recv()
        own[d, t] = own[d, t] + arrive[side, d, t]

    for i in range(Z - 1):
        du, dd = Z - 1 - i, i

        def step(t, carry):
            @pl.when(jnp.logical_and(z > 0, z < du))
            def _():
                pass_on(du, t, True)

            @pl.when(jnp.logical_and(z < du, z > (0 if i == 0 else -1)))
            def _():
                send_z(du, t, True).start()

            @pl.when(jnp.logical_and(z < Z - 1, z > dd))
            def _():
                pass_on(dd, t, False)

            @pl.when(jnp.logical_and(z > dd, z < (Z - 1 if i == 0 else Z)))
            def _():
                send_z(dd, t, False).start()
            return carry

        lax.fori_loop(0, T, step, 0)

    def to_peer(peer, t):
        return pltpu.make_async_remote_copy(
            src_ref=fin.at[peer, t], dst_ref=landed.at[g, t], send_sem=xsend.at[peer], recv_sem=xrecv.at[g],
            device_id={"gx": peer}, device_id_type=MESH)

    def close(t, carry):
        @pl.when(z > 0)
        def _():
            pass_on(z, t, True)

        @pl.when(z < Z - 1)
        def _():
            pass_on(z, t, False)

        total = own[z, t]
        for s in range(N):
            fin[s, t] = total[s * pk:(s + 1) * pk, :]
        for j in range(1, N):
            to_peer(lax.rem(g + j, N), t).start()
        return carry

    lax.fori_loop(0, T, close, 0)

    pair = [occ[pair_occ[k, 0]] + occ[pair_occ[k, 1]] for k in range(pk)]
    which = lax.broadcasted_iota(jnp.int32, (pk, W), 0)
    pe = jnp.zeros((pk, W), jnp.float32)
    for k in range(pk):
        pe = jnp.where(which == k, pair[k], pe)

    def finish(src, at):
        for t in range(T):
            cols = pl.ds(pl.multiple_of((at * T + t) * W, W), W)
            v = src[at, t]
            res_out[:, cols] = v
            upd_out[:, cols] = v / (ab_energy[:, cols] - pe)

    def whole(s):
        return pltpu.make_async_remote_copy(
            src_ref=fin.at[s], dst_ref=landed.at[s], send_sem=xsend.at[s], recv_sem=xrecv.at[s],
            device_id={"gx": s}, device_id_type=MESH)

    finish(fin, g)

    def collect(j, carry):
        s = lax.rem(g + j, N)
        whole(s).wait_recv()
        finish(landed, s)
        return carry

    lax.fori_loop(1, N, collect, 0)

    for peer in like:
        send_own(peer).wait_send()
        relay(peer).wait_send()
    send_own(partner).wait_send()

    def drain(j, carry):
        whole(lax.rem(g + j, N)).wait_send()
        return carry

    lax.fori_loop(1, N, drain, 0)
    for d in range(Z):
        @pl.when(z != d)
        def _():
            def drain_z(t, carry):
                send_z(d, t, True).wait_send()
                return carry
            lax.fori_loop(0, T, drain_z, 0)


def fused_body(N, Z, W, amplitudes, integrals, cd_irrep, ab_irrep, allowed, pair_occ, occ_energy, ab_energy):
    rows, K = amplitudes.shape
    AB = integrals.shape[1]
    A = ab_energy.shape[0]
    T = AB // W
    pk = rows // Z
    RP = N * pk
    PP = rows * N
    vmem, smem, hbm = pltpu.VMEM, pltpu.SMEM, pl.ANY
    f32, bf16 = jnp.float32, jnp.bfloat16
    dma = pltpu.SemaphoreType.DMA
    out = jax.ShapeDtypeStruct((pk, A), f32)
    return pl.pallas_call(
        functools.partial(kernel, N, Z, T, W),
        out_shape=(out, out),
        in_specs=[pl.BlockSpec(memory_space=s) for s in (vmem, hbm, smem, smem, smem, smem, smem, vmem)],
        out_specs=[pl.BlockSpec(memory_space=vmem)] * 2,
        scratch_shapes=[
            vmem((T, K, W), f32), vmem((T, K, W), bf16), vmem((T, K, W), bf16),
            vmem((N, rows, K), f32), vmem((PP, K), f32), vmem((2 * PP, K), bf16),
            vmem((Z, T, RP, W), f32), vmem((2, Z, T, RP, W), f32),
            vmem((N, T, pk, W), f32), vmem((N, T, pk, W), f32),
            dma((T,)), dma((N,)), dma((N,)), dma((N,)), dma((Z, T)), dma((2, Z, T)), dma((N,)), dma((N,)),
        ],
        compiler_params=pltpu.CompilerParams(
            collective_id=0, has_side_effects=True, vmem_limit_bytes=VMEM_BUDGET),
    )(amplitudes, integrals, cd_irrep, ab_irrep, allowed, pair_occ, occ_energy, ab_energy.reshape(1, A))


def solution(mesh):
    N, Z = mesh.shape["gx"], mesh.shape["row"]

    def body(amplitudes, integrals, *rest):
        rows, K = amplitudes.shape
        AB = integrals.shape[1]
        W = 2 * BLK
        pk = rows // Z
        need = 8 * K * AB + 16 * rows * N * K + 12 * rows * N * AB + 24 * pk * AB * N
        if need > VMEM_BUDGET * 3 // 4 or AB % W or N % 2 or rows % Z:
            return plain_body(amplitudes, integrals, *rest)
        return fused_body(N, Z, W, amplitudes, integrals, *rest)

    return jax.shard_map(
        body,
        mesh=mesh,
        in_specs=(
            P("gx", "row"),
            P("row", "gx"),
            P("row"),
            P("gx"),
            P(),
            P(("gx", "row"), None),
            P(),
            P(),
        ),
        out_specs=(P(("gx", "row"), None), P(("gx", "row"), None)),
        check_vma=False,
    )
```

```python
import functools

import jax
import jax.numpy as jnp
from jax import lax
from jax.experimental import pallas as pl
from jax.experimental.pallas import tpu as pltpu
from jax.sharding import PartitionSpec as P

BLK = 128
MESH = pl.DeviceIdType.MESH
VMEM_BUDGET = 48 * 2**20
VMEM_GRANT = 67043328


def plain_body(amplitudes, integrals, cd_irrep, ab_irrep, allowed, pair_occ, occ_energy, ab_energy):
    irrep_labels = jnp.arange(allowed.shape[0], dtype=jnp.int32)
    cd_onehot = (cd_irrep[:, None] == irrep_labels[None, :]).astype(jnp.float32)
    ab_onehot = (ab_irrep[:, None] == irrep_labels[None, :]).astype(jnp.float32)
    irrep_table = allowed.astype(jnp.float32)
    block_mask = jnp.dot(
        jnp.dot(cd_onehot, irrep_table, precision=lax.Precision.HIGHEST),
        ab_onehot.T,
        precision=lax.Precision.HIGHEST,
    )
    cd_rows, ab_cols = integrals.shape
    effective = (
        integrals.reshape(cd_rows // BLK, BLK, ab_cols // BLK, BLK) * block_mask[:, None, :, None]
    ).reshape(cd_rows, ab_cols)
    partial_value = jnp.dot(
        lax.all_gather(amplitudes, "gx", axis=0, tiled=True),
        effective,
        precision=lax.Precision.HIGHEST,
        preferred_element_type=jnp.float32,
    )
    arrived = lax.all_to_all(partial_value, "gx", split_axis=0, concat_axis=1, tiled=True)
    residual = lax.psum_scatter(arrived, "row", scatter_dimension=0, tiled=True)
    occ_labels = jnp.arange(occ_energy.shape[0], dtype=jnp.int32)
    pair_onehot = (pair_occ[:, :, None] == occ_labels[None, None, :]).astype(jnp.float32)
    pair_energy = jnp.sum(pair_onehot * occ_energy[None, None, :], axis=(1, 2))
    update = residual / (ab_energy[None, :] - pair_energy[:, None])
    return (residual, update)


def kernel(
    N, Z, T, W, L,
    amp, integ, cd_in, ab_in, allowed_in, pair_in, occ_in, energy_in,
    res_out, upd_out,
    cd, ab, allowed, pair_occ, occ, ab_energy, small_sem, amp_sem,
    raw, wh, wl, gathered, ordered, a2, own, arrive, fin, landed,
    isem, ag_send, ag_recv, relay_send, zsend, zrecv, xsend, xrecv,
):
    g = lax.axis_index("gx")
    z = lax.axis_index("row")
    rows, K = amp.shape
    PP = rows * N
    pk = rows // Z
    partner = g + 1 - 2 * lax.rem(g, 2)
    parity = lax.rem(g, 2)

    def load(t):
        cols = pl.ds(pl.multiple_of(t * W, W), W)
        return pltpu.make_async_copy(integ.at[:, cols], raw.at[t], isem.at[t])

    own_amp = pltpu.make_async_copy(amp, gathered.at[g], amp_sem)
    own_amp.start()
    small = [
        pltpu.make_async_copy(src, dst, small_sem.at[i])
        for i, (src, dst) in enumerate((
            (cd_in, cd), (ab_in, ab), (allowed_in, allowed), (pair_in, pair_occ), (occ_in, occ), (energy_in, ab_energy)))
    ]
    for c in small:
        c.start()
    for t in range(T):
        load(t).start()

    barrier = pltpu.get_barrier_semaphore()
    for j in range(1, N):
        pl.semaphore_signal(barrier, inc=1, device_id={"gx": lax.rem(g + j, N)}, device_id_type=MESH)

    @pl.when(z > 0)
    def _():
        pl.semaphore_signal(barrier, inc=1, device_id={"row": z - 1}, device_id_type=MESH)

    @pl.when(z < Z - 1)
    def _():
        pl.semaphore_signal(barrier, inc=1, device_id={"row": z + 1}, device_id_type=MESH)

    nearby = jnp.where(z > 0, 1, 0) + jnp.where(z < Z - 1, 1, 0)
    pl.semaphore_wait(barrier, N - 1 + nearby)

    def send_own(peer):
        return pltpu.make_async_remote_copy(
            src_ref=gathered.at[g], dst_ref=gathered.at[g], send_sem=ag_send.at[peer], recv_sem=ag_recv.at[g],
            device_id={"gx": peer}, device_id_type=MESH)

    def relay(s):
        return pltpu.make_async_remote_copy(
            src_ref=gathered.at[s], dst_ref=gathered.at[s], send_sem=relay_send.at[s], recv_sem=ag_recv.at[s],
            device_id={"gx": partner}, device_id_type=MESH)

    like = [lax.rem(g + 2 * j, N) for j in range(N // 2 - 1, 0, -1)]
    own_amp.wait()
    for peer in like:
        send_own(peer).start()
    send_own(partner).start()
    for c in small:
        c.wait()

    KB = K // BLK
    WB = W // BLK

    def split(t, carry):
        load(t).wait()
        for b in range(KB):
            for j in range(WB):
                m = allowed[cd[b], ab[t * WB + j]].astype(jnp.float32)
                x = raw[t, b * BLK:(b + 1) * BLK, j * BLK:(j + 1) * BLK] * m
                hi = x.astype(jnp.bfloat16)
                wh[t, b * BLK:(b + 1) * BLK, j * BLK:(j + 1) * BLK] = hi
                wl[t, b * BLK:(b + 1) * BLK, j * BLK:(j + 1) * BLK] = (x - hi.astype(jnp.float32)).astype(jnp.bfloat16)
        return carry

    lax.fori_loop(0, T, split, 0)

    for s in like[::-1]:
        relay(s).wait_recv()
        relay(s).start()
    relay(partner).wait_recv()
    for j in range(1, N // 2):
        relay(lax.rem(partner + 2 * j, N)).wait_recv()

    for r in range(Z):
        for s in range(N):
            at = r * N * pk + s * pk
            ordered[at:at + pk, :] = gathered[s, r * pk:(r + 1) * pk, :]
    x = ordered[...]
    hi = x.astype(jnp.bfloat16)
    a2[0:PP, :] = hi
    a2[PP:2 * PP, :] = (x - hi.astype(jnp.float32)).astype(jnp.bfloat16)

    RP = N * pk

    def send_z(d, t, up):
        to = z + 1 if up else z - 1
        side = 0 if up else 1
        return pltpu.make_async_remote_copy(
            src_ref=own.at[d, t], dst_ref=arrive.at[side, d, t], send_sem=zsend.at[d, t],
            recv_sem=zrecv.at[side, d, t], device_id={"row": to}, device_id_type=MESH)

    def compute(t):
        both = jnp.dot(a2[...], wh[t], preferred_element_type=jnp.float32)
        tail = jnp.dot(a2[0:PP, :], wl[t], preferred_element_type=jnp.float32)
        total = both[0:PP] + both[PP:2 * PP] + tail
        for d in range(Z):
            own[d, t] = total[d * RP:(d + 1) * RP, :]

    def take(d, t, up):
        side = 0 if up else 1
        send_z(d, t, up).wait_recv()
        own[d, t] = own[d, t] + arrive[side, d, t]

    def to_peer(peer, t):
        return pltpu.make_async_remote_copy(
            src_ref=fin.at[peer, t], dst_ref=landed.at[g, t], send_sem=xsend.at[peer], recv_sem=xrecv.at[g],
            device_id={"gx": peer}, device_id_type=MESH)

    def close(t):
        @pl.when(z > 0)
        def _():
            take(z, t, True)

        @pl.when(z < Z - 1)
        def _():
            take(z, t, False)

        total = own[z, t]
        for s in range(N):
            fin[s, t] = total[s * pk:(s + 1) * pk, :]
        for j in range(1, N):
            to_peer(lax.rem(g + j, N), t).start()

    last = Z - 1 - z
    lag_up, lag_down = z * L, last * L
    first_close = jnp.maximum(last * T + lag_up, z * T + lag_down)

    def step(s, carry):
        @pl.when(s < T)
        def _():
            compute(s)

        qu = s - lag_up

        @pl.when(jnp.logical_and(qu >= 0, qu < last * T))
        def _():
            d, t = Z - 1 - qu // T, lax.rem(qu, T)

            @pl.when(z > 0)
            def _():
                take(d, t, True)

            send_z(d, t, True).start()

        qd = s - lag_down

        @pl.when(jnp.logical_and(qd >= 0, qd < z * T))
        def _():
            d, t = qd // T, lax.rem(qd, T)

            @pl.when(z < Z - 1)
            def _():
                take(d, t, False)

            send_z(d, t, False).start()

        tc = s - first_close

        @pl.when(jnp.logical_and(tc >= 0, tc < T))
        def _():
            close(tc)

        return carry

    lax.fori_loop(0, Z * T + (Z - 1) * L, step, 0)

    pair = [occ[pair_occ[0, k]] + occ[pair_occ[1, k]] for k in range(pk)]
    which = lax.broadcasted_iota(jnp.int32, (pk, W), 0)
    pe = jnp.zeros((pk, W), jnp.float32)
    for k in range(pk):
        pe = jnp.where(which == k, pair[k], pe)

    def finish(src, at):
        for t in range(T):
            cols = pl.ds(pl.multiple_of((at * T + t) * W, W), W)
            v = src[at, t]
            res_out[:, cols] = v
            upd_out[:, cols] = v / (ab_energy[:, cols] - pe)

    def whole(s):
        return pltpu.make_async_remote_copy(
            src_ref=fin.at[s], dst_ref=landed.at[s], send_sem=xsend.at[s], recv_sem=xrecv.at[s],
            device_id={"gx": s}, device_id_type=MESH)

    finish(fin, g)

    def collect(j, carry):
        s = lax.rem(g + j, N)
        whole(s).wait_recv()
        finish(landed, s)
        return carry

    lax.fori_loop(1, N, collect, 0)

    for peer in like:
        send_own(peer).wait_send()
        relay(peer).wait_send()
    send_own(partner).wait_send()

    def drain(j, carry):
        whole(lax.rem(g + j, N)).wait_send()
        return carry

    lax.fori_loop(1, N, drain, 0)
    for d in range(Z):
        @pl.when(z != d)
        def _():
            def drain_z(t, carry):
                send_z(d, t, True).wait_send()
                return carry
            lax.fori_loop(0, T, drain_z, 0)


def fused_body(N, Z, W, L, amplitudes, integrals, cd_irrep, ab_irrep, allowed, pair_occ, occ_energy, ab_energy):
    rows, K = amplitudes.shape
    AB = integrals.shape[1]
    A = ab_energy.shape[0]
    T = AB // W
    pk = rows // Z
    RP = N * pk
    PP = rows * N
    vmem, smem = pltpu.VMEM, pltpu.SMEM
    f32, bf16, i32 = jnp.float32, jnp.bfloat16, jnp.int32
    dma = pltpu.SemaphoreType.DMA
    out = jax.ShapeDtypeStruct((pk, A), f32)
    return pl.pallas_call(
        functools.partial(kernel, N, Z, T, W, L),
        out_shape=(out, out),
        in_specs=[pl.BlockSpec(memory_space=pltpu.HBM)] * 8,
        out_specs=[pl.BlockSpec(memory_space=vmem)] * 2,
        scratch_shapes=[
            smem(cd_irrep.shape, i32), smem(ab_irrep.shape, i32), smem(allowed.shape, i32),
            smem(pair_occ.shape[::-1], i32), smem(occ_energy.shape, f32), vmem((1, A), f32), dma((6,)), dma,
            vmem((T, K, W), f32), vmem((T, K, W), bf16), vmem((T, K, W), bf16),
            vmem((N, rows, K), f32), vmem((PP, K), f32), vmem((2 * PP, K), bf16),
            vmem((Z, T, RP, W), f32), vmem((2, Z, T, RP, W), f32),
            vmem((N, T, pk, W), f32), vmem((N, T, pk, W), f32),
            dma((T,)), dma((N,)), dma((N,)), dma((N,)), dma((Z, T)), dma((2, Z, T)), dma((N,)), dma((N,)),
        ],
        compiler_params=pltpu.CompilerParams(
            collective_id=0, has_side_effects=True, vmem_limit_bytes=VMEM_GRANT),
    )(amplitudes, integrals, cd_irrep, ab_irrep, allowed, pair_occ.T, occ_energy, ab_energy.reshape(1, A))


def solution(mesh):
    N, Z = mesh.shape["gx"], mesh.shape["row"]

    def body(amplitudes, integrals, *rest):
        rows, K = amplitudes.shape
        AB = integrals.shape[1]
        W = 2 * BLK
        pk = rows // Z
        need = 8 * K * AB + 16 * rows * N * K + 12 * rows * N * AB + 24 * pk * AB * N
        if need > VMEM_BUDGET * 3 // 4 or AB % W or N % 2 or rows % Z:
            return plain_body(amplitudes, integrals, *rest)
        return fused_body(N, Z, W, 3, amplitudes, integrals, *rest)

    return jax.shard_map(
        body,
        mesh=mesh,
        in_specs=(
            P("gx", "row"),
            P("row", "gx"),
            P("row"),
            P("gx"),
            P(),
            P(("gx", "row"), None),
            P(),
            P(),
        ),
        out_specs=(P(("gx", "row"), None), P(("gx", "row"), None)),
        check_vma=False,
    )
```

```python
import functools

import jax
import jax.numpy as jnp
from jax import lax
from jax.experimental import pallas as pl
from jax.experimental.pallas import tpu as pltpu
from jax.sharding import PartitionSpec as P

BLK = 128
MESH = pl.DeviceIdType.MESH
VMEM_BUDGET = 48 * 2**20
VMEM_GRANT = 67043328


def plain_body(amplitudes, integrals, cd_irrep, ab_irrep, allowed, pair_occ, occ_energy, ab_energy):
    irrep_labels = jnp.arange(allowed.shape[0], dtype=jnp.int32)
    cd_onehot = (cd_irrep[:, None] == irrep_labels[None, :]).astype(jnp.float32)
    ab_onehot = (ab_irrep[:, None] == irrep_labels[None, :]).astype(jnp.float32)
    irrep_table = allowed.astype(jnp.float32)
    block_mask = jnp.dot(
        jnp.dot(cd_onehot, irrep_table, precision=lax.Precision.HIGHEST),
        ab_onehot.T,
        precision=lax.Precision.HIGHEST,
    )
    cd_rows, ab_cols = integrals.shape
    effective = (
        integrals.reshape(cd_rows // BLK, BLK, ab_cols // BLK, BLK) * block_mask[:, None, :, None]
    ).reshape(cd_rows, ab_cols)
    partial_value = jnp.dot(
        lax.all_gather(amplitudes, "gx", axis=0, tiled=True),
        effective,
        precision=lax.Precision.HIGHEST,
        preferred_element_type=jnp.float32,
    )
    arrived = lax.all_to_all(partial_value, "gx", split_axis=0, concat_axis=1, tiled=True)
    residual = lax.psum_scatter(arrived, "row", scatter_dimension=0, tiled=True)
    occ_labels = jnp.arange(occ_energy.shape[0], dtype=jnp.int32)
    pair_onehot = (pair_occ[:, :, None] == occ_labels[None, None, :]).astype(jnp.float32)
    pair_energy = jnp.sum(pair_onehot * occ_energy[None, None, :], axis=(1, 2))
    update = residual / (ab_energy[None, :] - pair_energy[:, None])
    return (residual, update)


def kernel(
    N, Z, T, W, L,
    amp, integ, cd_in, ab_in, allowed_in,
    res_out,
    cd, ab, allowed, small_sem, amp_sem,
    raw, wh, wl, gathered, ordered, a2, own, arrive, fin,
    isem, ag_send, ag_recv, relay_send, zsend, zrecv, xsend, xrecv, own_sem,
):
    g = lax.axis_index("gx")
    z = lax.axis_index("row")
    rows, K = amp.shape
    half, Zh = rows // 2, Z // 2
    HP = half * N
    pk = rows // Z
    far = jnp.where(z < Zh, 1, 0)
    partner = g + 1 - 2 * lax.rem(g, 2)
    parity = lax.rem(g, 2)

    def load(t):
        cols = pl.ds(pl.multiple_of(t * W, W), W)
        return pltpu.make_async_copy(integ.at[:, cols], raw.at[t], isem.at[t])

    def own_amp(h):
        return pltpu.make_async_copy(
            amp.at[pl.ds(pl.multiple_of(h * half, half), half), :], gathered.at[g, h], amp_sem.at[h])

    own_amp(far).start()
    own_amp(1 - far).start()
    small = [
        pltpu.make_async_copy(src, dst, small_sem.at[i])
        for i, (src, dst) in enumerate((
            (cd_in, cd), (ab_in, ab), (allowed_in, allowed)))
    ]
    for c in small:
        c.start()
    for t in range(T):
        load(t).start()

    barrier = pltpu.get_barrier_semaphore()
    for j in range(1, N):
        pl.semaphore_signal(barrier, inc=1, device_id={"gx": lax.rem(g + j, N)}, device_id_type=MESH)

    @pl.when(z > 0)
    def _():
        pl.semaphore_signal(barrier, inc=1, device_id={"row": z - 1}, device_id_type=MESH)

    @pl.when(z < Z - 1)
    def _():
        pl.semaphore_signal(barrier, inc=1, device_id={"row": z + 1}, device_id_type=MESH)

    nearby = jnp.where(z > 0, 1, 0) + jnp.where(z < Z - 1, 1, 0)
    pl.semaphore_wait(barrier, N - 1 + nearby)

    def send_own(peer, h):
        return pltpu.make_async_remote_copy(
            src_ref=gathered.at[g, h], dst_ref=gathered.at[g, h], send_sem=ag_send.at[h, peer],
            recv_sem=ag_recv.at[h, g], device_id={"gx": peer}, device_id_type=MESH)

    def relay(s, h):
        return pltpu.make_async_remote_copy(
            src_ref=gathered.at[s, h], dst_ref=gathered.at[s, h], send_sem=relay_send.at[h, s],
            recv_sem=ag_recv.at[h, s], device_id={"gx": partner}, device_id_type=MESH)

    like = [lax.rem(g + 2 * j, N) for j in range(N // 2 - 1, 0, -1)]
    for h in (far, 1 - far):
        own_amp(h).wait()
        for peer in like:
            send_own(peer, h).start()
        send_own(partner, h).start()
    for c in small:
        c.wait()

    KB = K // BLK
    WB = W // BLK

    def split(t, carry):
        load(t).wait()
        for b in range(KB):
            for j in range(WB):
                m = allowed[cd[b], ab[t * WB + j]].astype(jnp.float32)
                x = raw[t, b * BLK:(b + 1) * BLK, j * BLK:(j + 1) * BLK] * m
                hi = x.astype(jnp.bfloat16)
                wh[t, b * BLK:(b + 1) * BLK, j * BLK:(j + 1) * BLK] = hi
                wl[t, b * BLK:(b + 1) * BLK, j * BLK:(j + 1) * BLK] = (x - hi.astype(jnp.float32)).astype(jnp.bfloat16)
        return carry

    lax.fori_loop(0, T, split, 0)

    def forward(h):
        for s in like[::-1]:
            relay(s, h).wait_recv()
            relay(s, h).start()

    def prepare(h):
        relay(partner, h).wait_recv()
        for j in range(1, N // 2):
            relay(lax.rem(partner + 2 * j, N), h).wait_recv()
        for r in range(Zh):
            for s in range(N):
                at = (r * N + s) * pk
                ordered[at:at + pk, :] = gathered[s, h, r * pk:(r + 1) * pk, :]
        x = ordered[...]
        hi = x.astype(jnp.bfloat16)
        a2[0:HP, :] = hi
        a2[HP:2 * HP, :] = (x - hi.astype(jnp.float32)).astype(jnp.bfloat16)

    forward(far)
    prepare(far)

    RP = N * pk

    def send_z(d, t, up):
        to = z + 1 if up else z - 1
        side = 0 if up else 1
        return pltpu.make_async_remote_copy(
            src_ref=own.at[d, t], dst_ref=arrive.at[side, d, t], send_sem=zsend.at[d, t],
            recv_sem=zrecv.at[side, d, t], device_id={"row": to}, device_id_type=MESH)

    def compute(t, h):
        both = jnp.dot(a2[...], wh[t], preferred_element_type=jnp.float32)
        tail = jnp.dot(a2[0:HP, :], wl[t], preferred_element_type=jnp.float32)
        total = both[0:HP] + both[HP:2 * HP] + tail
        for r in range(Zh):
            own[h * Zh + r, t] = total[r * RP:(r + 1) * RP, :]

    def take(d, t, up):
        side = 0 if up else 1
        send_z(d, t, up).wait_recv()
        own[d, t] = own[d, t] + arrive[side, d, t]

    def place(s, t):
        return pl.ds(pl.multiple_of((s * T + t) * W, W), W)

    def keep(t):
        return pltpu.make_async_copy(fin.at[g, t], res_out.at[:, place(g, t)], own_sem.at[t])

    def to_peer(peer, t):
        return pltpu.make_async_remote_copy(
            src_ref=fin.at[peer, t], dst_ref=res_out.at[:, place(g, t)], send_sem=xsend.at[peer], recv_sem=xrecv.at[g],
            device_id={"gx": peer}, device_id_type=MESH)

    def close(t):
        @pl.when(z > 0)
        def _():
            take(z, t, True)

        @pl.when(z < Z - 1)
        def _():
            take(z, t, False)

        total = own[z, t]
        for s in range(N):
            fin[s, t] = total[s * pk:(s + 1) * pk, :]
        for j in range(1, N):
            to_peer(lax.rem(g + j, N), t).start()
        keep(t).start()

    last = Z - 1 - z
    lag_up, lag_down = z * L, last * L
    first_close = jnp.maximum(last * T + lag_up, z * T + lag_down)

    def step(s, carry):
        @pl.when(s == T // 4)
        def _():
            forward(1 - far)

        @pl.when(s == T)
        def _():
            prepare(1 - far)

        @pl.when(s < 2 * T)
        def _():
            compute(lax.rem(s, T), jnp.where(s < T, far, 1 - far))

        qu = s - lag_up

        @pl.when(jnp.logical_and(qu >= 0, qu < last * T))
        def _():
            d, t = Z - 1 - qu // T, lax.rem(qu, T)

            @pl.when(z > 0)
            def _():
                take(d, t, True)

            send_z(d, t, True).start()

        qd = s - lag_down

        @pl.when(jnp.logical_and(qd >= 0, qd < z * T))
        def _():
            d, t = qd // T, lax.rem(qd, T)

            @pl.when(z < Z - 1)
            def _():
                take(d, t, False)

            send_z(d, t, False).start()

        tc = s - first_close

        @pl.when(jnp.logical_and(tc >= 0, tc < T))
        def _():
            close(tc)

        return carry

    lax.fori_loop(0, Z * T + (Z - 1) * L, step, 0)

    def whole(s):
        band = res_out.at[:, pl.ds(pl.multiple_of(s * T * W, W), T * W)]
        return pltpu.make_async_remote_copy(
            src_ref=band, dst_ref=band, send_sem=xsend.at[s], recv_sem=xrecv.at[s],
            device_id={"gx": s}, device_id_type=MESH)

    for peer in like:
        for h in range(2):
            send_own(peer, h).wait_send()
            relay(peer, h).wait_send()
    for h in range(2):
        send_own(partner, h).wait_send()

    def collect(j, carry):
        whole(lax.rem(g + j, N)).wait_recv()
        return carry

    lax.fori_loop(1, N, collect, 0)

    def drain_own(t, carry):
        keep(t).wait()
        return carry

    lax.fori_loop(0, T, drain_own, 0)

    def drain(j, carry):
        whole(lax.rem(g + j, N)).wait_send()
        return carry

    lax.fori_loop(1, N, drain, 0)
    for d in range(Z):
        @pl.when(z != d)
        def _():
            def drain_z(t, carry):
                send_z(d, t, True).wait_send()
                return carry
            lax.fori_loop(0, T, drain_z, 0)


def divide(res, pair_occ, occ, energy, res_out, upd_out):
    pk, A = res.shape
    which = lax.broadcasted_iota(jnp.int32, (pk, 1), 0)
    pe = jnp.zeros((pk, 1), jnp.float32)
    for k in range(pk):
        pe = jnp.where(which == k, occ[pair_occ[0, k]] + occ[pair_occ[1, k]], pe)
    v = res[...]
    res_out[...] = v
    upd_out[...] = v / (energy[...] - pe)


def fused_body(N, Z, W, L, amplitudes, integrals, cd_irrep, ab_irrep, allowed, pair_occ, occ_energy, ab_energy):
    rows, K = amplitudes.shape
    AB = integrals.shape[1]
    A = ab_energy.shape[0]
    T = AB // W
    pk = rows // Z
    RP = N * pk
    HP = rows * N // 2
    vmem, smem = pltpu.VMEM, pltpu.SMEM
    f32, bf16, i32 = jnp.float32, jnp.bfloat16, jnp.int32
    dma = pltpu.SemaphoreType.DMA
    out = jax.ShapeDtypeStruct((pk, A), f32)
    residual = pl.pallas_call(
        functools.partial(kernel, N, Z, T, W, L),
        out_shape=out,
        in_specs=[pl.BlockSpec(memory_space=pltpu.HBM)] * 5,
        out_specs=pl.BlockSpec(memory_space=pltpu.HBM),
        scratch_shapes=[
            smem(cd_irrep.shape, i32), smem(ab_irrep.shape, i32), smem(allowed.shape, i32), dma((3,)), dma((2,)),
            vmem((T, K, W), f32), vmem((T, K, W), bf16), vmem((T, K, W), bf16),
            vmem((N, 2, rows // 2, K), f32), vmem((HP, K), f32), vmem((2 * HP, K), bf16),
            vmem((Z, T, RP, W), f32), vmem((2, Z, T, RP, W), f32), vmem((N, T, pk, W), f32),
            dma((T,)), dma((2, N)), dma((2, N)), dma((2, N)), dma((Z, T)), dma((2, Z, T)), dma((N,)), dma((N,)),
            dma((T,)),
        ],
        compiler_params=pltpu.CompilerParams(
            collective_id=0, has_side_effects=True, vmem_limit_bytes=VMEM_GRANT),
    )(amplitudes, integrals, cd_irrep, ab_irrep, allowed)
    return pl.pallas_call(
        divide,
        out_shape=(out, out),
        in_specs=[pl.BlockSpec(memory_space=s) for s in (vmem, smem, smem, vmem)],
        out_specs=[pl.BlockSpec(memory_space=vmem)] * 2,
        compiler_params=pltpu.CompilerParams(vmem_limit_bytes=VMEM_GRANT),
    )(residual, pair_occ.T, occ_energy, ab_energy.reshape(1, A))


def solution(mesh):
    N, Z = mesh.shape["gx"], mesh.shape["row"]

    def body(amplitudes, integrals, *rest):
        rows, K = amplitudes.shape
        AB = integrals.shape[1]
        W = 2 * BLK
        L = max(3, pl.cdiv(2 * (AB // W), Z))
        pk = rows // Z
        need = 8 * K * AB + 16 * rows * N * K + 12 * rows * N * AB + 24 * pk * AB * N
        if need > VMEM_BUDGET * 3 // 4 or AB % W or N % 2 or Z % 2 or rows % Z or rows % 16:
            return plain_body(amplitudes, integrals, *rest)
        return fused_body(N, Z, W, L, amplitudes, integrals, *rest)

    return jax.shard_map(
        body,
        mesh=mesh,
        in_specs=(
            P("gx", "row"),
            P("row", "gx"),
            P("row"),
            P("gx"),
            P(),
            P(("gx", "row"), None),
            P(),
            P(),
        ),
        out_specs=(P(("gx", "row"), None), P(("gx", "row"), None)),
        check_vma=False,
    )
```

```python
import functools

import jax
import jax.numpy as jnp
from jax import lax
from jax.experimental import pallas as pl
from jax.experimental.pallas import tpu as pltpu
from jax.sharding import PartitionSpec as P

BLK = 128
MESH = pl.DeviceIdType.MESH
VMEM_BUDGET = 48 * 2**20
VMEM_GRANT = 67043328


def plain_body(amplitudes, integrals, cd_irrep, ab_irrep, allowed, pair_occ, occ_energy, ab_energy):
    irrep_labels = jnp.arange(allowed.shape[0], dtype=jnp.int32)
    cd_onehot = (cd_irrep[:, None] == irrep_labels[None, :]).astype(jnp.float32)
    ab_onehot = (ab_irrep[:, None] == irrep_labels[None, :]).astype(jnp.float32)
    irrep_table = allowed.astype(jnp.float32)
    block_mask = jnp.dot(
        jnp.dot(cd_onehot, irrep_table, precision=lax.Precision.HIGHEST),
        ab_onehot.T,
        precision=lax.Precision.HIGHEST,
    )
    cd_rows, ab_cols = integrals.shape
    effective = (
        integrals.reshape(cd_rows // BLK, BLK, ab_cols // BLK, BLK) * block_mask[:, None, :, None]
    ).reshape(cd_rows, ab_cols)
    partial_value = jnp.dot(
        lax.all_gather(amplitudes, "gx", axis=0, tiled=True),
        effective,
        precision=lax.Precision.HIGHEST,
        preferred_element_type=jnp.float32,
    )
    arrived = lax.all_to_all(partial_value, "gx", split_axis=0, concat_axis=1, tiled=True)
    residual = lax.psum_scatter(arrived, "row", scatter_dimension=0, tiled=True)
    occ_labels = jnp.arange(occ_energy.shape[0], dtype=jnp.int32)
    pair_onehot = (pair_occ[:, :, None] == occ_labels[None, None, :]).astype(jnp.float32)
    pair_energy = jnp.sum(pair_onehot * occ_energy[None, None, :], axis=(1, 2))
    update = residual / (ab_energy[None, :] - pair_energy[:, None])
    return (residual, update)


def kernel(
    N, Z, T, W, L,
    amp, integ, cd_in, ab_in, allowed_in,
    res_out,
    cd, ab, allowed, small_sem, amp_sem,
    raw, wh, wl, gathered, ordered, a2, own, arrive, fin,
    isem, ag_send, ag_recv, relay_send, zsend, zrecv, xsend, xrecv, own_sem,
):
    g = lax.axis_index("gx")
    z = lax.axis_index("row")
    rows, K = amp.shape
    half, Zh = rows // 2, Z // 2
    HP = half * N
    pk = rows // Z
    far = jnp.where(z < Zh, 1, 0)
    partner = g + 1 - 2 * lax.rem(g, 2)
    parity = lax.rem(g, 2)

    def load(t):
        cols = pl.ds(pl.multiple_of(t * W, W), W)
        return pltpu.make_async_copy(integ.at[:, cols], raw.at[t], isem.at[t])

    def own_amp(h):
        return pltpu.make_async_copy(
            amp.at[pl.ds(pl.multiple_of(h * half, half), half), :], gathered.at[g, h], amp_sem.at[h])

    own_amp(far).start()
    own_amp(1 - far).start()
    small = [
        pltpu.make_async_copy(src, dst, small_sem.at[i])
        for i, (src, dst) in enumerate((
            (cd_in, cd), (ab_in, ab), (allowed_in, allowed)))
    ]
    for c in small:
        c.start()
    barrier = pltpu.get_barrier_semaphore()
    for j in range(1, N):
        pl.semaphore_signal(barrier, inc=1, device_id={"gx": lax.rem(g + j, N)}, device_id_type=MESH)

    @pl.when(z > 0)
    def _():
        pl.semaphore_signal(barrier, inc=1, device_id={"row": z - 1}, device_id_type=MESH)

    @pl.when(z < Z - 1)
    def _():
        pl.semaphore_signal(barrier, inc=1, device_id={"row": z + 1}, device_id_type=MESH)

    nearby = jnp.where(z > 0, 1, 0) + jnp.where(z < Z - 1, 1, 0)
    pl.semaphore_wait(barrier, N - 1 + nearby)

    def send_own(peer, h):
        return pltpu.make_async_remote_copy(
            src_ref=gathered.at[g, h], dst_ref=gathered.at[g, h], send_sem=ag_send.at[h, peer],
            recv_sem=ag_recv.at[h, g], device_id={"gx": peer}, device_id_type=MESH)

    def relay(s, h):
        return pltpu.make_async_remote_copy(
            src_ref=gathered.at[s, h], dst_ref=gathered.at[s, h], send_sem=relay_send.at[h, s],
            recv_sem=ag_recv.at[h, s], device_id={"gx": partner}, device_id_type=MESH)

    like = [lax.rem(g + 2 * j, N) for j in range(N // 2 - 1, 0, -1)]
    for h in (far, 1 - far):
        own_amp(h).wait()
        for peer in like:
            send_own(peer, h).start()
        send_own(partner, h).start()
    for t in range(T):
        load(t).start()
    for c in small:
        c.wait()

    KB = K // BLK
    WB = W // BLK

    def split(t, carry):
        load(t).wait()
        for b in range(KB):
            for j in range(WB):
                m = allowed[cd[b], ab[t * WB + j]].astype(jnp.float32)
                x = raw[t, b * BLK:(b + 1) * BLK, j * BLK:(j + 1) * BLK] * m
                hi = x.astype(jnp.bfloat16)
                wh[t, b * BLK:(b + 1) * BLK, j * BLK:(j + 1) * BLK] = hi
                wl[t, b * BLK:(b + 1) * BLK, j * BLK:(j + 1) * BLK] = (x - hi.astype(jnp.float32)).astype(jnp.bfloat16)
        return carry

    lax.fori_loop(0, T, split, 0)

    def forward(h):
        for s in like[::-1]:
            relay(s, h).wait_recv()
            relay(s, h).start()

    def prepare(h):
        relay(partner, h).wait_recv()
        for j in range(1, N // 2):
            relay(lax.rem(partner + 2 * j, N), h).wait_recv()
        for r in range(Zh):
            for s in range(N):
                at = (r * N + s) * pk
                ordered[at:at + pk, :] = gathered[s, h, r * pk:(r + 1) * pk, :]
        x = ordered[...]
        hi = x.astype(jnp.bfloat16)
        a2[0:HP, :] = hi
        a2[HP:2 * HP, :] = (x - hi.astype(jnp.float32)).astype(jnp.bfloat16)

    forward(far)
    prepare(far)

    RP = N * pk

    def send_z(d, t, up):
        to = z + 1 if up else z - 1
        side = 0 if up else 1
        return pltpu.make_async_remote_copy(
            src_ref=own.at[d, t], dst_ref=arrive.at[side, d, t], send_sem=zsend.at[d, t],
            recv_sem=zrecv.at[side, d, t], device_id={"row": to}, device_id_type=MESH)

    def compute(t, h):
        both = jnp.dot(a2[...], wh[t], preferred_element_type=jnp.float32)
        tail = jnp.dot(a2[0:HP, :], wl[t], preferred_element_type=jnp.float32)
        total = both[0:HP] + both[HP:2 * HP] + tail
        for r in range(Zh):
            own[h * Zh + r, t] = total[r * RP:(r + 1) * RP, :]

    def take(d, t, up):
        side = 0 if up else 1
        send_z(d, t, up).wait_recv()
        own[d, t] = own[d, t] + arrive[side, d, t]

    def place(s, t):
        return pl.ds(pl.multiple_of((s * T + t) * W, W), W)

    def keep(t):
        return pltpu.make_async_copy(fin.at[g, t], res_out.at[:, place(g, t)], own_sem.at[t])

    def to_peer(peer, t):
        return pltpu.make_async_remote_copy(
            src_ref=fin.at[peer, t], dst_ref=res_out.at[:, place(g, t)], send_sem=xsend.at[peer], recv_sem=xrecv.at[g],
            device_id={"gx": peer}, device_id_type=MESH)

    def close(t):
        @pl.when(z > 0)
        def _():
            take(z, t, True)

        @pl.when(z < Z - 1)
        def _():
            take(z, t, False)

        total = own[z, t]
        for s in range(N):
            fin[s, t] = total[s * pk:(s + 1) * pk, :]
        for j in range(1, N):
            to_peer(lax.rem(g + j, N), t).start()
        keep(t).start()

    last = Z - 1 - z
    lag_up, lag_down = z * L, last * L
    first_close = jnp.maximum(last * T + lag_up, z * T + lag_down)

    def step(s, carry):
        @pl.when(s == T // 4)
        def _():
            forward(1 - far)

        @pl.when(s == T)
        def _():
            prepare(1 - far)

        @pl.when(s < 2 * T)
        def _():
            compute(lax.rem(s, T), jnp.where(s < T, far, 1 - far))

        qu = s - lag_up

        @pl.when(jnp.logical_and(qu >= 0, qu < last * T))
        def _():
            d, t = Z - 1 - qu // T, lax.rem(qu, T)

            @pl.when(z > 0)
            def _():
                take(d, t, True)

            send_z(d, t, True).start()

        qd = s - lag_down

        @pl.when(jnp.logical_and(qd >= 0, qd < z * T))
        def _():
            d, t = qd // T, lax.rem(qd, T)

            @pl.when(z < Z - 1)
            def _():
                take(d, t, False)

            send_z(d, t, False).start()

        tc = s - first_close

        @pl.when(jnp.logical_and(tc >= 0, tc < T))
        def _():
            close(tc)

        return carry

    lax.fori_loop(0, Z * T + (Z - 1) * L, step, 0)

    def whole(s):
        band = res_out.at[:, pl.ds(pl.multiple_of(s * T * W, W), T * W)]
        return pltpu.make_async_remote_copy(
            src_ref=band, dst_ref=band, send_sem=xsend.at[s], recv_sem=xrecv.at[s],
            device_id={"gx": s}, device_id_type=MESH)

    for peer in like:
        for h in range(2):
            send_own(peer, h).wait_send()
            relay(peer, h).wait_send()
    for h in range(2):
        send_own(partner, h).wait_send()

    def collect(j, carry):
        whole(lax.rem(g + j, N)).wait_recv()
        return carry

    lax.fori_loop(1, N, collect, 0)

    def drain_own(t, carry):
        keep(t).wait()
        return carry

    lax.fori_loop(0, T, drain_own, 0)

    def drain(j, carry):
        whole(lax.rem(g + j, N)).wait_send()
        return carry

    lax.fori_loop(1, N, drain, 0)
    for d in range(Z):
        @pl.when(z != d)
        def _():
            def drain_z(t, carry):
                send_z(d, t, True).wait_send()
                return carry
            lax.fori_loop(0, T, drain_z, 0)


def divide(res, pair_occ, occ, energy, res_out, upd_out):
    pk, A = res.shape
    which = lax.broadcasted_iota(jnp.int32, (pk, 1), 0)
    pe = jnp.zeros((pk, 1), jnp.float32)
    for k in range(pk):
        pe = jnp.where(which == k, occ[pair_occ[0, k]] + occ[pair_occ[1, k]], pe)
    v = res[...]
    res_out[...] = v
    upd_out[...] = v / (energy[...] - pe)


def fused_body(N, Z, W, L, amplitudes, integrals, cd_irrep, ab_irrep, allowed, pair_occ, occ_energy, ab_energy):
    rows, K = amplitudes.shape
    AB = integrals.shape[1]
    A = ab_energy.shape[0]
    T = AB // W
    pk = rows // Z
    RP = N * pk
    HP = rows * N // 2
    vmem, smem = pltpu.VMEM, pltpu.SMEM
    f32, bf16, i32 = jnp.float32, jnp.bfloat16, jnp.int32
    dma = pltpu.SemaphoreType.DMA
    out = jax.ShapeDtypeStruct((pk, A), f32)
    residual = pl.pallas_call(
        functools.partial(kernel, N, Z, T, W, L),
        out_shape=out,
        in_specs=[pl.BlockSpec(memory_space=pltpu.HBM)] * 5,
        out_specs=pl.BlockSpec(memory_space=pltpu.HBM),
        scratch_shapes=[
            smem(cd_irrep.shape, i32), smem(ab_irrep.shape, i32), smem(allowed.shape, i32), dma((3,)), dma((2,)),
            vmem((T, K, W), f32), vmem((T, K, W), bf16), vmem((T, K, W), bf16),
            vmem((N, 2, rows // 2, K), f32), vmem((HP, K), f32), vmem((2 * HP, K), bf16),
            vmem((Z, T, RP, W), f32), vmem((2, Z, T, RP, W), f32), vmem((N, T, pk, W), f32),
            dma((T,)), dma((2, N)), dma((2, N)), dma((2, N)), dma((Z, T)), dma((2, Z, T)), dma((N,)), dma((N,)),
            dma((T,)),
        ],
        compiler_params=pltpu.CompilerParams(
            collective_id=0, has_side_effects=True, vmem_limit_bytes=VMEM_GRANT),
    )(amplitudes, integrals, cd_irrep, ab_irrep, allowed)
    return pl.pallas_call(
        divide,
        out_shape=(out, out),
        in_specs=[pl.BlockSpec(memory_space=s) for s in (vmem, smem, smem, vmem)],
        out_specs=[pl.BlockSpec(memory_space=vmem)] * 2,
        compiler_params=pltpu.CompilerParams(vmem_limit_bytes=VMEM_GRANT),
    )(residual, pair_occ.T, occ_energy, ab_energy.reshape(1, A))


def solution(mesh):
    N, Z = mesh.shape["gx"], mesh.shape["row"]

    def body(amplitudes, integrals, *rest):
        rows, K = amplitudes.shape
        AB = integrals.shape[1]
        W = 2 * BLK
        L = max(3, pl.cdiv(2 * (AB // W), Z))
        pk = rows // Z
        need = 8 * K * AB + 16 * rows * N * K + 12 * rows * N * AB + 24 * pk * AB * N
        if need > VMEM_BUDGET * 3 // 4 or AB % W or N % 2 or Z % 2 or rows % Z or rows % 16:
            return plain_body(amplitudes, integrals, *rest)
        return fused_body(N, Z, W, L, amplitudes, integrals, *rest)

    return jax.shard_map(
        body,
        mesh=mesh,
        in_specs=(
            P("gx", "row"),
            P("row", "gx"),
            P("row"),
            P("gx"),
            P(),
            P(("gx", "row"), None),
            P(),
            P(),
        ),
        out_specs=(P(("gx", "row"), None), P(("gx", "row"), None)),
        check_vma=False,
    )
```
